32 devices in a mesh: dp: 2 (over y), row: 4 (over x, core), col: 4 (over z).
Axes of the slice: x: 2, y: 2, z: 4, core: 2. Of those that a mesh axis runs over, the one named last changes fastest.
Arguments:
- inputs: bfloat16 [4096, 1024], P(('dp', 'row'), 'col'), may hold values from -6 to 6
- cotangent: bfloat16 [4096, 1024], P(('dp', 'row'), 'col'), may hold values from -6 to 6
- mixer_in: bfloat16 [1024, 4120], P('col', 'row'), may hold values from -0.1875 to 0.1875
- mixer_out: bfloat16 [2048, 1024], P('row', 'col'), may hold values from -0.1875 to 0.1875
- expand_weight: bfloat16 [1024, 4096], P('col', 'row'), may hold values from -0.1875 to 0.1875
- shrink_weight: bfloat16 [2048, 1024], P('row', 'col'), may hold values from -0.125 to 0.125
- input_gain: float32 [1024], P('col'), may hold values from 0.1 to 1.9
- middle_gain: float32 [1024], P('col'), may hold values from 0.1 to 1.9
- mixer_kernel: float32 [4, 1536], P(None, 'row'), may hold values from -3 to 3
- shared_kernel: float32 [4, 256], replicated, may hold values from -3 to 3
- decay_log: float32 [24], P('row'), may hold values from -4 to 0.5
- step_bias: float32 [24], P('row'), may hold values from -4 to -1
- skip_scale: float32 [24], P('row'), may hold values from 0.5 to 2
- state_gain: float32 [1536], P('row'), may hold values from 0.1 to 1.9
- dealing: int32 [4, 4, 2], replicated, may hold values from 0 to 1, as said below
- lengths: int32 [4, 2, 4, 4], replicated, may hold values from 1 to 96, 128 in all within a row
Outputs:
- outputs: bfloat16 [4096, 1024], P(('dp', 'row'), 'col')
- input_grad: bfloat16 [4096, 1024], P(('dp', 'row'), 'col')
- mixer_in_grad: float32 [1024, 4120], P('col', 'row')
- mixer_out_grad: float32 [2048, 1024], P('row', 'col')
- expand_grad: float32 [1024, 4096], P('col', 'row')
- shrink_grad: float32 [2048, 1024], P('row', 'col')
- input_gain_grad: float32 [1024], P('col')
- middle_gain_grad: float32 [1024], P('col')
- mixer_kernel_grad: float32 [4, 1536], P(None, 'row')
- shared_kernel_grad: float32 [4, 256], replicated
- decay_log_grad: float32 [24], P('row')
- step_bias_grad: float32 [24], P('row')
- skip_scale_grad: float32 [24], P('row')
- state_gain_grad: float32 [1536], P('row')
The draws below stay inside these ranges and needn't reach their ends.
Inputs may be any that keep to these rules, and one draw needn't show every extreme that they name: For every micro-batch m and slot r, dealing[m, r] is a permutation of the 2 groups. For every slot r and sending group g, no group receives more than ceil(2) of g's 4 packs in slot r. lengths[m, e, r] lists in order the 4 sequences of the pack that group e holds in slot r of micro-batch m; they sum to 128.
All inputs are finite; a program needn't handle non-finite values.
Results may differ from the reference program's by a relative error of at most 0.019.
Values may be sent and summed in bfloat16 or wider, within the bound.
No kernel may reach another device: no remote copies, remote signals or barrier semaphores. Data moves between devices by JAX's collectives and lax.ppermute only.
A program may use at most 128 MiB of HBM per device.

```python
import math
import jax
import jax.numpy as jnp
import numpy as np
from jax import lax

D = 1024
QUERY_HEADS = 8
KEY_VALUE_HEADS = 2
HEAD_WIDTH = 64
NM = 24
MD = 64
STATE_WIDTH = 128
KC = 4
FF = 2048
PACK_TOKENS = 128
MB = 4
NSEQ = 4
DS = 1536
GROUPS = 2
SLOTS = 4
TOKENS = 4096
BLK = 1030
PROJ = 4120
MIXW = 2048
LONGEST = 96
N_ROW = 4


def draw_dealing(key, part):

    def one_slot(slot_key):
        first_key, second_key = jax.random.split(slot_key)
        ordering = jax.random.permutation(first_key, GROUPS)
        labels = jax.random.permutation(second_key, GROUPS)
        micro_ids = jnp.arange(MB, dtype=jnp.int32)
        return labels[(ordering[None, :] + micro_ids[:, None]) % GROUPS]
    slot_keys = jax.random.split(jax.random.fold_in(key, 7), SLOTS)
    dealt_all = jax.vmap(one_slot)(slot_keys)
    return jnp.transpose(dealt_all, (1, 0, 2)).astype(jnp.int32)


def shard_levels(stream_key, dims, pieces, smallest, high):
    level = 1.0
    for position, parts in pieces:
        draws = jax.random.uniform(jax.random.fold_in(jax.random.fold_in(stream_key, 6), position), (parts,), jnp.float32, smallest / len(pieces), high / len(pieces))
        level = level * jnp.repeat(jnp.exp(draws), dims[position] // parts).reshape((-1,) + (1,) * (len(dims) - 1 - position))
    return level


def split_up(count, total, limit, lean):
    loads = [(1 << 20) // math.isqrt(standing ** lean) + 1 for standing in range(2, count + 1)]
    spare, given = total - limit - (count - 1), [1] * (count - 1)
    while spare > 0:
        movable = [i for i in range(count - 1) if given[i] < limit]
        pool, budget = sum([loads[i] for i in movable]), spare
        for i in movable:
            addition = min(limit - given[i], max(1, budget * loads[i] // pool), spare)
            given[i] = given[i] + addition
            spare = spare - addition
    return np.array([limit] + given)


def ragged_sizes(own_key, number_of, total, reach, skew):
    if number_of == 2:
        one = jax.random.randint(own_key, (), max(1, total - reach), min(reach, total - 1) + 1)
        return jnp.stack([one, total - one])
    tallies = jnp.asarray(split_up(number_of, total, reach, skew), jnp.int32)
    pairs = (number_of - 1) // 2
    giver, sink = tallies[1:1 + 2 * pairs:2], tallies[2:2 + 2 * pairs:2]
    room = jnp.minimum(giver - 1, reach - sink)
    moved = jax.random.randint(jax.random.fold_in(own_key, 1), (pairs,), 0, 1 << 20) % (room + 1)
    tallies = tallies.at[1:1 + 2 * pairs:2].set(giver - moved).at[2:2 + 2 * pairs:2].set(sink + moved)
    return tallies[jax.random.permutation(jax.random.fold_in(own_key, 2), number_of)]


def gaussian(stream_key, extent, scale, reach, cuts=(), held_as=jnp.bfloat16):
    level = shard_levels(stream_key, extent, cuts, -0.22, 0.18) if cuts else 1.0
    drawn = jax.random.normal(stream_key, extent, jnp.float32) * scale * level
    return jnp.minimum(jnp.maximum(drawn, -reach), reach).astype(held_as)


def setup_inputs(seed: int = 0) -> dict:
    seeds = jax.random.split(jax.random.key(seed), 17)
    return {
        "inputs": gaussian(seeds[0], (TOKENS, D), 1.0, 6.0, ((0, 8), (1, 4))),
        "cotangent": gaussian(seeds[1], (TOKENS, D), 1.0, 6.0, ((0, 8), (1, 4))),
        "mixer_in": gaussian(seeds[2], (D, PROJ), D ** -0.5, 0.1875, ((0, 4), (1, 4))),
        "mixer_out": gaussian(seeds[3], (MIXW, D), D ** -0.5, 0.1875, ((0, 4), (1, 4))),
        "expand_weight": gaussian(seeds[4], (D, 2 * FF), D ** -0.5, 0.1875, ((0, 4), (1, 4))),
        "shrink_weight": gaussian(seeds[5], (FF, D), FF ** -0.5, 0.125, ((0, 4), (1, 4))),
        "input_gain": jnp.clip(1.0 + 0.18 * jax.random.normal(seeds[6], (D,), jnp.float32), 0.1, 1.9),
        "middle_gain": jnp.clip(1.0 + 0.18 * jax.random.normal(seeds[7], (D,), jnp.float32), 0.1, 1.9),
        "mixer_kernel": gaussian(seeds[8], (KC, DS), 0.5, 3.0, ((1, 4),), jnp.float32),
        "shared_kernel": gaussian(seeds[9], (KC, 2 * STATE_WIDTH), 0.5, 3.0, (), jnp.float32),
        "decay_log": jnp.clip(-4.0 + 4.5 * jax.random.uniform(seeds[10], (NM,), jnp.float32) ** shard_levels(seeds[10], (NM,), ((0, 4),), -0.2, 0.2), -4.0, 0.5),
        "step_bias": jnp.clip(-4.0 + 3.0 * jax.random.uniform(seeds[11], (NM,), jnp.float32) ** shard_levels(seeds[11], (NM,), ((0, 4),), -0.2, 0.2), -4.0, -1.0),
        "skip_scale": jnp.clip(0.5 + 1.5 * jax.random.uniform(seeds[12], (NM,), jnp.float32) ** shard_levels(seeds[12], (NM,), ((0, 4),), -0.2, 0.2), 0.5, 2.0),
        "state_gain": jnp.clip(1.0 + 0.18 * jax.random.normal(seeds[13], (DS,), jnp.float32), 0.1, 1.9),
        "dealing": draw_dealing(jax.random.fold_in(seeds[16], 71), 0),
        "lengths": jax.vmap(lambda own: ragged_sizes(own, NSEQ, PACK_TOKENS, LONGEST, 1))(jax.random.split(seeds[15], MB * GROUPS * SLOTS)).reshape((MB, GROUPS, SLOTS, NSEQ)).astype(jnp.int32),
    }


@jax.custom_vjp
def low(v):
    return lax.optimization_barrier(v.astype(jnp.bfloat16)).astype(jnp.float32)

@jax.custom_vjp
def low_back(v):
    return v

def low_keep(v):
    return (low(v), None)

def low_pass(kept, grad):
    return (grad,)

def back_keep(v):
    return (v, None)

def back_low(kept, grad):
    return (low(grad),)
low.defvjp(low_keep, low_pass)
low_back.defvjp(back_keep, back_low)
epsilon = 1e-05
masked_value = -1e+30
rope_base = 10000.0

def matmul(left, right):
    return jnp.dot(left, right, precision=lax.Precision.HIGHEST, preferred_element_type=jnp.float32)

def rms_scale(values, gain):
    return values * lax.rsqrt(lax.optimization_barrier(jnp.mean(values * values, axis=-1, keepdims=True)) + epsilon) * gain

def segment_info(lengths_row, count_of_rows):
    seg_ends = jnp.cumsum(lengths_row).astype(jnp.int32)
    places = jnp.arange(count_of_rows, dtype=jnp.int32)
    segment = lax.optimization_barrier(jnp.sum((places[:, None] >= seg_ends[None, :]).astype(jnp.int32), axis=1)).astype(jnp.int32)
    starts = (seg_ends - lengths_row).astype(jnp.int32)
    onehot = segment[:, None] == jnp.arange(lengths_row.shape[0], dtype=jnp.int32)[None, :]
    token_position = (places - lax.optimization_barrier(jnp.sum(jnp.where(onehot, starts[None, :], 0), axis=1))).astype(jnp.int32)
    return (segment, token_position)

def apply_rotary(values, token_position, direction):
    half_dim = values.shape[-1] // 2
    frequency = rope_base ** (-jnp.arange(half_dim, dtype=jnp.float32) * 2.0 / values.shape[-1])
    angles = token_position.astype(jnp.float32)[:, None] * frequency[None, :]
    cosine = jnp.cos(angles)[:, None, :]
    sine_part = direction * jnp.sin(angles)[:, None, :]
    first_half = values[..., :half_dim]
    second = values[..., half_dim:]
    return jnp.concatenate([first_half * cosine - second * sine_part, second * cosine + first_half * sine_part], axis=-1)

def causal_conv(values, kernel, segment):
    summed = values * kernel[0][None, :]
    for offset in range(1, kernel.shape[0]):
        shifted = jnp.concatenate([jnp.zeros((offset, values.shape[1]), values.dtype), values[:-offset]], axis=0)
        earlier = jnp.concatenate([jnp.full((offset,), -1, jnp.int32), segment[:-offset]], axis=0)
        summed = summed + jnp.where((earlier == segment)[:, None], shifted, 0.0) * kernel[offset][None, :]
    return summed

def layer(inputs, params, segment, token_position):
    mixer_in, mixer_out, expand_weight, shrink_weight, input_gain, middle_gain, mixer_kernel, shared_kernel, decay_log, step_bias, skip_scale, state_gain = params
    count_of_rows = inputs.shape[0]
    query_w = QUERY_HEADS * HEAD_WIDTH // N_ROW
    shared_w = 4 * STATE_WIDTH // N_ROW
    inner_w = DS // N_ROW
    places = jnp.arange(count_of_rows, dtype=jnp.int32)
    allowed = (segment[:, None] == segment[None, :]) & (places[:, None] >= places[None, :])
    normed = low(rms_scale(inputs, input_gain))
    blocks = low_back(matmul(normed, mixer_in)).reshape(count_of_rows, N_ROW, BLK)
    queries = blocks[:, :, :query_w].reshape(count_of_rows, QUERY_HEADS, HEAD_WIDTH)
    common_projection = blocks[:, :, query_w:query_w + shared_w].reshape(count_of_rows, 4 * STATE_WIDTH)
    gate_start = query_w + shared_w
    gate_raw = blocks[:, :, gate_start:gate_start + inner_w].reshape(count_of_rows, DS)
    inner_raw = blocks[:, :, gate_start + inner_w:gate_start + 2 * inner_w].reshape(count_of_rows, DS)
    step_raw = blocks[:, :, gate_start + 2 * inner_w:].reshape(count_of_rows, NM)
    key_matrix = apply_rotary(common_projection[:, :STATE_WIDTH].reshape(count_of_rows, KEY_VALUE_HEADS, HEAD_WIDTH), token_position, 1.0).reshape(count_of_rows, STATE_WIDTH)
    states = jax.nn.silu(causal_conv(common_projection[:, 2 * STATE_WIDTH:], shared_kernel, segment))
    dispatched = low(jnp.concatenate([key_matrix, common_projection[:, STATE_WIDTH:2 * STATE_WIDTH], states], axis=1))
    key_head_rows = dispatched[:, :STATE_WIDTH].reshape(count_of_rows, KEY_VALUE_HEADS, HEAD_WIDTH)
    value_head_rows = dispatched[:, STATE_WIDTH:2 * STATE_WIDTH].reshape(count_of_rows, KEY_VALUE_HEADS, HEAD_WIDTH)
    in_state = dispatched[:, 2 * STATE_WIDTH:3 * STATE_WIDTH]
    out_state = dispatched[:, 3 * STATE_WIDTH:]
    queries = low(apply_rotary(queries, token_position, 1.0))
    score_scale = HEAD_WIDTH ** (-0.5)
    queries_per_key = QUERY_HEADS // KEY_VALUE_HEADS

    def attend(head_index):
        query_head = lax.dynamic_index_in_dim(queries, head_index, 1, False)
        key_head = lax.dynamic_index_in_dim(key_head_rows, head_index // queries_per_key, 1, False)
        value_head = lax.dynamic_index_in_dim(value_head_rows, head_index // queries_per_key, 1, False)
        scores = low_back(matmul(query_head, key_head.T) * score_scale)
        masked = jnp.where(allowed, scores, masked_value)
        exponent = jnp.exp(masked - lax.optimization_barrier(jnp.max(masked, axis=1, keepdims=True)))
        probability = low(exponent / lax.optimization_barrier(jnp.sum(exponent, axis=1, keepdims=True)))
        return matmul(probability, value_head)
    attended = jnp.transpose(lax.map(jax.checkpoint(attend), jnp.arange(QUERY_HEADS)), (1, 0, 2))
    attended = low_back(attended).reshape(count_of_rows, N_ROW, query_w)
    conv_out = jax.nn.silu(causal_conv(inner_raw, mixer_kernel, segment))
    step_size = jax.nn.softplus(step_raw + step_bias[None, :])
    decay_rates = -jnp.exp(decay_log)
    cumulative = jnp.cumsum(step_size * decay_rates[None, :], axis=0)
    intersection = matmul(out_state, in_state.T)

    def scan_head(head_index):
        cum_head = lax.dynamic_index_in_dim(cumulative, head_index, 1, False)
        decay = jnp.exp(jnp.where(allowed, cum_head[:, None] - cum_head[None, :], masked_value))
        mixing = low(decay * low_back(intersection))
        conv_head = lax.dynamic_slice_in_dim(conv_out, head_index * MD, MD, 1)
        driven = low(conv_head * lax.dynamic_index_in_dim(step_size, head_index, 1, False)[:, None])
        skip_head = lax.dynamic_index_in_dim(skip_scale, head_index, 0, False)
        return low_back(matmul(mixing, driven)) + skip_head * conv_head
    state_out = jnp.transpose(lax.map(jax.checkpoint(scan_head), jnp.arange(NM)), (1, 0, 2)).reshape(count_of_rows, DS)
    gated = state_out * jax.nn.silu(gate_raw)
    state_normed = rms_scale(gated, state_gain).reshape(count_of_rows, N_ROW, inner_w)
    mixed = low(jnp.concatenate([attended, state_normed], axis=2).reshape(count_of_rows, MIXW))
    middle = inputs + low_back(matmul(mixed, mixer_out))
    normed2 = low(rms_scale(middle, middle_gain))
    expanded = low_back(matmul(normed2, expand_weight)).reshape(count_of_rows, N_ROW, 2, FF // N_ROW)
    hidden = low(jax.nn.silu(expanded[:, :, 0]) * expanded[:, :, 1]).reshape(count_of_rows, FF)
    return middle + low_back(matmul(hidden, shrink_weight))

def reference(inputs, cotangent, mixer_in, mixer_out, expand_weight, shrink_weight, input_gain, middle_gain, mixer_kernel, shared_kernel, decay_log, step_bias, skip_scale, state_gain, dealing, lengths):
    group_ids = jnp.arange(GROUPS, dtype=jnp.int32)
    matches = dealing[:, :, :, None] == group_ids[None, None, None, :]
    source = lax.optimization_barrier(jnp.sum(jnp.where(matches, group_ids[None, None, :, None], 0), axis=2)).astype(jnp.int32)
    micro_ids = jnp.arange(MB, dtype=jnp.int32)
    slot_ids = jnp.arange(SLOTS, dtype=jnp.int32)

    def to_packs(array):
        arrived = array.astype(jnp.float32).reshape(GROUPS, SLOTS, MB, PACK_TOKENS, D)
        picked = arrived[source, slot_ids[None, :, None], micro_ids[:, None, None]]
        return jnp.transpose(picked, (0, 2, 1, 3, 4)).reshape(MB * GROUPS * SLOTS, PACK_TOKENS, D)

    def to_order(packs):
        shaped = packs.reshape(MB, GROUPS, SLOTS, PACK_TOKENS, D)
        destination = jnp.transpose(dealing, (2, 1, 0))
        returned = shaped[micro_ids[None, None, :], destination, slot_ids[None, :, None]]
        return returned.reshape(TOKENS, D)
    weights = tuple((weight_item.astype(jnp.float32) for weight_item in (mixer_in, mixer_out, expand_weight, shrink_weight, input_gain, middle_gain, mixer_kernel, shared_kernel, decay_log, step_bias, skip_scale, state_gain)))
    pack_lengths = lengths.reshape(MB * GROUPS * SLOTS, NSEQ)

    def one_pack(carried, entry):
        pack_in, pack_cot, pack_len = entry
        segment, token_position = segment_info(pack_len, PACK_TOKENS)

        def forward_pass(values, params):
            return layer(values, params, segment, token_position)
        result, pullback = jax.vjp(forward_pass, pack_in, weights)
        grad_in, grad_params = pullback(pack_cot)
        carried = tuple((first_item + second_item for first_item, second_item in zip(carried, grad_params)))
        return (carried, (result.astype(jnp.bfloat16), grad_in.astype(jnp.bfloat16)))
    zeros = tuple((jnp.zeros(weight_item.shape, jnp.float32) for weight_item in weights))
    grads, (results, input_grads) = lax.scan(one_pack, zeros, (to_packs(inputs), to_packs(cotangent), pack_lengths))
    return (to_order(results), to_order(input_grads), grads[0], grads[1], grads[2], grads[3], grads[4], grads[5], grads[6], grads[7], grads[8], grads[9], grads[10], grads[11])
```

```python
import jax
import jax.numpy as jnp
from jax import lax
from jax.experimental import pallas as pl
from jax.experimental.pallas import tpu as pltpu
from jax.sharding import PartitionSpec as P

D = 1024
QUERY_HEADS = 8
KEY_VALUE_HEADS = 2
HEAD_WIDTH = 64
NM = 24
MD = 64
STATE_WIDTH = 128
KC = 4
FF = 2048
T = 128
MB = 4
DS = 1536
SLOTS = 4
TT = SLOTS * T
QW = 128
IW = 384
HW = 512
PAIRS = 3
EPS = 1e-05
NEG = -1e30
ROPE_BASE = 10000.0
F32 = jnp.float32
BF = jnp.bfloat16
HI = lax.Precision.HIGHEST


def nn(a, b):
    return lax.dot_general(a, b, (((1,), (0,)), ((), ())), preferred_element_type=F32)


def nt(a, b):
    return lax.dot_general(a, b, (((1,), (1,)), ((), ())), preferred_element_type=F32)


def tn(a, b):
    return lax.dot_general(a, b, (((0,), (0,)), ((), ())), preferred_element_type=F32)


def nn_exact(a, b):
    return lax.dot_general(
        a, b, (((1,), (0,)), ((), ())), precision=HI, preferred_element_type=F32
    )


def lanes(rows=T):
    return lax.broadcasted_iota(jnp.int32, (rows, 128), 1)


def rows_of(j, n=T):
    return slice(j * n, (j + 1) * n)


def sigmoid(v):
    return 1.0 / (1.0 + jnp.exp(-v))


def silu_slope(v, s):
    return s * (1.0 + v * (1.0 - s))


def swap_halves(v):
    lane = lanes(v.shape[0])
    return jnp.where((lane % 64) < 32, pltpu.roll(v, 96, 1), pltpu.roll(v, 32, 1))


def conv(v, k, pos):
    acc = v * k[0:1]
    for j in range(1, KC):
        acc = acc + jnp.where(pos >= j, pltpu.roll(v, j, 0), 0.0) * k[j : j + 1]
    return acc


def tile_lanes(v, n):
    return jnp.concatenate([v] * n, axis=1)


def conv_back(dcv, v, k, pos):
    n = v.shape[0]
    dv = dcv * k[0:1]
    dk = [jnp.sum(dcv * v, axis=0, keepdims=True)]
    for j in range(1, KC):
        m = jnp.where(pos >= j, dcv, 0.0)
        dv = dv + pltpu.roll(m, n - j, 0) * k[j : j + 1]
        dk.append(jnp.sum(m * pltpu.roll(v, j, 0), axis=0, keepdims=True))
    return dv, dk


def hi_lo(total):
    wide = jnp.broadcast_to(total, (total.shape[0], 128))
    high = wide.astype(BF).astype(F32)
    return jnp.where(lanes(total.shape[0]) < 64, high, wide - high).astype(BF)


def from_hi_lo(v):
    v = v.astype(F32)
    return v + pltpu.roll(v, 64, 1)


def pick(scal, pieces, block, j):
    k_of = scal[0] ^ block
    out = pieces[0][rows_of(j)].astype(F32)
    for k in range(1, SLOTS):
        out = jnp.where(k_of == k, pieces[k][rows_of(j ^ k)].astype(F32), out)
    return out


def both_heads(v, kv):
    keep = (lanes(v.shape[0]) // 64) == kv
    return jnp.where(keep, v, pltpu.roll(v, 64, 1))


def split_pair(v):
    low = lanes(v.shape[0]) < 64
    zero = jnp.zeros_like(v)
    return jnp.concatenate([jnp.where(low, v, zero), jnp.where(low, zero, v)], axis=0)


def join_pair(v):
    n = v.shape[0] // 2
    return jnp.where(lanes(n) < 64, v[:n], v[n:])


def fold_pair(v, kv):
    total = v + pltpu.roll(v, 64, 1)
    return jnp.where((lanes(v.shape[0]) // 64) == kv, total, 0.0)


def mask_of(pos):
    ti = lax.broadcasted_iota(jnp.int32, (T, T), 0)
    si = lax.broadcasted_iota(jnp.int32, (T, T), 1)
    d = (ti - si).astype(F32)
    return (d >= 0) & (d <= pos)


def head_col(v, h):
    return jnp.broadcast_to(v[:, h : h + 1], (v.shape[0], 128))


def pair_cols(v, k):
    return jnp.where(lanes(v.shape[0]) < 64, head_col(v, 2 * k), head_col(v, 2 * k + 1))


def tri(upper):
    a = lax.broadcasted_iota(jnp.int32, (T, T), 0)
    b = lax.broadcasted_iota(jnp.int32, (T, T), 1)
    return jnp.where((b >= a) if upper else (b <= a), 1.0, 0.0).astype(F32)


def prep_body(scal, own, peer, gain, x_ref, n_ref, inv_ref):
    mine = scal[1] == 1
    total = jnp.zeros((T, 1), F32)
    for c in range(4):
        v = jnp.where(mine, own[c].astype(F32), peer[c].astype(F32))
        x_ref[:, c * 256 : (c + 1) * 256] = v.astype(BF)
        total = total + jnp.sum(v * v, axis=1, keepdims=True)
    inv = lax.rsqrt(total / D + EPS)
    inv_ref[...] = jnp.broadcast_to(inv, (T, 128))
    n_ref[...] = (x_ref[...].astype(F32) * inv * gain[...]).astype(BF)


def proj1_body(scal, x0, x1, x2, x3, w, pos, cs, sn, kc, x_ref, q_ref, raw_ref, sh_ref):
    for j, piece in enumerate((x0, x1, x2, x3)):
        x_ref[rows_of(j)] = piece[...]
    qs = nn(x_ref[...], w[:, 0:256])
    r = scal[0]
    for j in range(SLOTS):
        rr = rows_of(j)
        q = qs[rr, 0:128]
        v = qs[rr, 128:256]
        q_ref[rr] = (q * cs[rr] + swap_halves(q) * sn[rr]).astype(BF)
        raw_ref[rr] = v
        rotated = v * cs[rr] + swap_halves(v) * sn[rr]
        cv = conv(v, kc[...], pos[rr])
        act = cv * sigmoid(cv)
        sh_ref[rr] = jnp.where(r == 0, rotated, jnp.where(r >= 2, act, v)).astype(BF)


def proj2_body(x, w, pos, mk, bias, z_ref, u_ref, w_ref, cv_ref):
    for n in range(3):
        res = nn(x[...], w[:, 256 * (n + 1) : 256 * (n + 2)])
        for half in range(2):
            part = res[:, half * 128 : (half + 1) * 128]
            i = 2 * n + half
            if i < 3:
                z_ref[:, i * 128 : (i + 1) * 128] = part
            else:
                i = i - 3
                cc = slice(i * 128, (i + 1) * 128)
                u_ref[:, cc] = part
                for j in range(SLOTS):
                    rr = rows_of(j)
                    cv_ref[rr, cc] = conv(part[rr], mk[:, cc], pos[rr])
    w_ref[...] = jnp.zeros_like(w_ref)
    w_ref[:, 0:6] = nn(x[...], w[:, 1024:1030])
    w_ref[...] = w_ref[...] + bias[...]


def softplus(v):
    return jnp.maximum(v, 0.0) + jnp.log1p(jnp.exp(-jnp.abs(v)))


def mixf_body(
    scal, q, p0, p1, p2, p3, pos, z, cv, wi, rate, skip, gain, wo,
    att_ref, prob_ref, state_ref, send_ref, keep_ref, gg_ref, st_ref,
):
    pieces = (p0, p1, p2, p3)
    kv = scal[0] // 2
    low = tri(False)
    for j in range(SLOTS):
        rr = rows_of(j)
        allowed = mask_of(pos[rr])
        allowed2 = jnp.concatenate([allowed, allowed], axis=0)
        keys = both_heads(pick(scal, pieces, 0, j), kv).astype(BF)
        vals = both_heads(pick(scal, pieces, 1, j), kv).astype(BF)
        q2 = split_pair(q[rr].astype(F32)).astype(BF)
        score = jnp.where(allowed2, nt(q2, keys) * (HEAD_WIDTH**-0.5), NEG)
        e = jnp.exp(score - jnp.max(score, axis=1, keepdims=True))
        prob = e / jnp.sum(e, axis=1, keepdims=True)
        prob_ref[rows_of(j, 2 * T)] = prob
        att_ref[rr] = join_pair(nn(prob.astype(BF), vals)).astype(BF)
        b_in = pick(scal, pieces, 2, j).astype(BF)
        c_out = pick(scal, pieces, 3, j).astype(BF)
        inter = nt(c_out, b_in)
        step = softplus(wi[rr])
        cum = nn_exact(low, step * rate[...])
        cum_t = jnp.transpose(cum)
        total = jnp.zeros((T, 128), F32)
        for k in range(PAIRS):
            cc = slice(k * 128, (k + 1) * 128)
            mix = []
            for h in (2 * k, 2 * k + 1):
                gap = head_col(cum, h) - cum_t[h : h + 1, :]
                mix.append((jnp.exp(jnp.where(allowed, gap, NEG)) * inter).astype(BF))
            c = cv[rr, cc]
            inner = c * sigmoid(c)
            driven = (inner * pair_cols(step, k)).astype(BF)
            state = join_pair(nn(jnp.concatenate(mix, axis=0), driven)) + skip[:, cc] * inner
            state_ref[rr, cc] = state
            zz = z[rr, cc]
            gated = state * (zz * sigmoid(zz))
            total = total + gated * gated
            gg_ref[rr, cc] = (gated * gain[:, cc]).astype(BF)
        st_ref[rr] = jnp.sum(total, axis=1, keepdims=True) + jnp.zeros((T, 128), F32)
    for c in range(4):
        pa = nn(att_ref[...], wo[c, 0:128, :])
        ps = nn(gg_ref[...], wo[c, 128:512, :])
        for off, part in ((0, pa), (1024, ps)):
            cc = slice(off + c * 256, off + (c + 1) * 256)
            for i in range(2):
                keep_ref[i, :, cc] = part[rows_of(2 * i)]
                send_ref[i, :, cc] = part[rows_of(2 * i + 1)].astype(BF)
    for i in range(2):
        keep_ref[i, :, 2048:2176] = hi_lo(st_ref[rows_of(2 * i), 0:1]).astype(F32)
        send_ref[i, :, 2048:2176] = hi_lo(st_ref[rows_of(2 * i + 1), 0:1])


def rsa_body(keep, recv, s0_ref, s2_ref):
    s0_ref[...] = keep[0] + recv[0].astype(F32)
    total = keep[1] + recv[1].astype(F32)
    width = s2_ref.shape[1]
    s2_ref[...] = total.astype(BF)
    if width == 2176:
        st = from_hi_lo(total[:, 2048:2176])
        s2_ref[:, 2048:2176] = hi_lo(st[:, 0:1])


def mid_body(s0, recv, x, gain, mid_ref, n_ref, zs_ref, inv_ref):
    zs = s0[:, 1024:2048] + recv[:, 1024:2048].astype(F32)
    st = from_hi_lo(s0[:, 2048:2176]) + from_hi_lo(recv[:, 2048:2176])
    scale = lax.rsqrt(st[:, 0:1] / DS + EPS)
    zs_ref[...] = zs
    mid = x[...].astype(F32) + s0[:, 0:1024] + recv[:, 0:1024].astype(F32) + scale * zs
    mid_ref[...] = mid
    inv = lax.rsqrt(jnp.sum(mid * mid, axis=1, keepdims=True) / D + EPS)
    inv_ref[...] = jnp.broadcast_to(inv, (T, 128))
    n_ref[:, 0:1024] = (mid * inv * gain[...]).astype(BF)
    n_ref[:, 1024:1152] = hi_lo(scale)


def ffn_body(
    n0, n1, n2, n3, y0, y1, y2, y3, we, ws,
    x_ref, y_ref, is_ref, h_ref, de_ref, send_ref, keep_ref,
):
    for j, (n, y) in enumerate(((n0, y0), (n1, y1), (n2, y2), (n3, y3))):
        rr = rows_of(j)
        x_ref[rr] = n[:, 0:1024]
        is_ref[rr] = from_hi_lo(n[:, 1024:1152])
        y_ref[rr] = y[...]
    for n in range(2):
        cc = slice(n * 256, (n + 1) * 256)
        uc = slice(HW + n * 256, HW + (n + 1) * 256)
        g = nn(x_ref[...], we[:, cc])
        u = nn(x_ref[...], we[:, uc])
        dh = jnp.zeros((TT, 256), F32)
        for c in range(4):
            dh = dh + nt(y_ref[:, c * 256 : (c + 1) * 256], ws[c, cc, :])
        s = sigmoid(g)
        act = g * s
        h_ref[:, cc] = (act * u).astype(BF)
        de_ref[:, cc] = (dh * u * silu_slope(g, s)).astype(BF)
        de_ref[:, uc] = (dh * act).astype(BF)
    for c in range(4):
        cc = slice(c * 256, (c + 1) * 256)
        part = nt(de_ref[...], we[cc, :])
        for i in range(2):
            keep_ref[i, :, cc] = part[rows_of(2 * i)]
            send_ref[i, :, cc] = part[rows_of(2 * i + 1)].astype(BF)


def outp_body(h, ws, send_ref, keep_ref):
    for c in range(4):
        cc = slice(c * 256, (c + 1) * 256)
        part = nn(h[...], ws[c])
        for i in range(2):
            keep_ref[i, :, cc] = part[rows_of(2 * i)]
            send_ref[i, :, cc] = part[rows_of(2 * i + 1)].astype(BF)


def fin_body(s0, recv, mid, o_ref):
    o_ref[...] = (mid[...] + s0[...] + recv[...].astype(F32)).astype(BF)


def dmid_body(s0, recv, mid, inv, dy, gain, zs, dm_ref, db_ref, gg_ref):
    dn = s0[...] + recv[...].astype(F32)
    m = mid[...]
    i2 = inv[:, 0:1]
    g = gain[...]
    inner = jnp.sum(dn * g * m, axis=1, keepdims=True)
    dm = dy[...].astype(F32) + i2 * g * dn - m * (i2 * i2 * i2 * inner / D)
    dm_ref[...] = dm
    gg_ref[...] = jnp.sum(dn * m * i2, axis=0, keepdims=True)
    db = dm.astype(BF)
    db_ref[:, 0:1024] = db
    db_ref[:, 1024:1152] = hi_lo(jnp.sum(db.astype(F32) * zs[...], axis=1, keepdims=True))


def mixb_body(
    scal, b0, b1, b2, b3, q, p0, p1, p2, p3, pos, cs, sn, prob, z, u, cv, state, wi, isb,
    att, rate, skip, gain, mk, wo,
    d_ref, mixed_ref, dq_ref, dz_ref, du_ref, dw_ref, send_ref, keep_ref,
    dmk_ref, dgain_ref, dskip_ref, dlog_ref, dbias_ref,
    dmix, blocks,
):
    pieces = (p0, p1, p2, p3)
    r = scal[0]
    kv = r // 2
    low, up = tri(False), tri(True)
    seg_row = lax.broadcasted_iota(jnp.int32, (IW, 128), 0) // 64
    seg_col = lax.broadcasted_iota(jnp.int32, (IW, 128), 1)
    heads = jnp.where(seg_row == seg_col, 1.0, 0.0).astype(F32)
    dmk_ref[...] = jnp.zeros_like(dmk_ref)
    dgain_ref[...] = jnp.zeros_like(dgain_ref)
    dskip_ref[...] = jnp.zeros_like(dskip_ref)
    dlog_ref[...] = jnp.zeros_like(dlog_ref)
    dbias_ref[...] = jnp.zeros_like(dbias_ref)
    for j, b in enumerate((b0, b1, b2, b3)):
        d_ref[rows_of(j)] = b[:, 0:1024]
    for n in range(2):
        cc = slice(n * 256, (n + 1) * 256)
        acc = jnp.zeros((TT, 256), F32)
        for c in range(4):
            acc = acc + nt(d_ref[:, c * 256 : (c + 1) * 256], wo[c, cc, :])
        dmix[:, cc] = acc
    for j, b in enumerate((b0, b1, b2, b3)):
        rr = rows_of(j)
        r2 = rows_of(j, 2 * T)
        allowed = mask_of(pos[rr])
        keys = both_heads(pick(scal, pieces, 0, j), kv).astype(BF)
        vals = both_heads(pick(scal, pieces, 1, j), kv).astype(BF)
        q2 = split_pair(q[rr].astype(F32)).astype(BF)
        da2 = split_pair(dmix[rr, 0:128]).astype(BF)
        pf = prob[r2]
        dprob = nt(da2, vals)
        delta = jnp.sum(dprob * pf, axis=1, keepdims=True)
        dscore = (pf * (dprob - delta)).astype(BF)
        scale = HEAD_WIDTH**-0.5
        dqr = join_pair(nn(dscore, keys)) * scale
        dq_ref[rr] = (dqr * cs[rr] - swap_halves(dqr) * sn[rr]).astype(BF)
        blocks[0] = fold_pair(tn(dscore, q2) * scale, kv)
        blocks[1] = fold_pair(tn(pf.astype(BF), da2), kv)
        b_in = pick(scal, pieces, 2, j).astype(BF)
        c_out = pick(scal, pieces, 3, j).astype(BF)
        inter = nt(c_out, b_in)
        sin = wi[rr]
        step = softplus(sin)
        cum = nn_exact(low, step * rate[...])
        cum_t = jnp.transpose(cum)
        scale_s = isb[rr, 0:1]
        inner_s = from_hi_lo(b[:, 1024:1152])[:, 0:1]
        coef = scale_s * scale_s * scale_s * inner_s / DS
        dinter = jnp.zeros((T, T), F32)
        dstep = jnp.zeros((T, 128), F32)
        dcum = jnp.zeros((T, 128), F32)
        mixed_ref[rr, 0:128] = att[rr]
        for k in range(PAIRS):
            cc = slice(k * 128, (k + 1) * 128)
            mc = slice((k + 1) * 128, (k + 2) * 128)
            c = cv[rr, cc]
            sc = sigmoid(c)
            inner = c * sc
            step_k = pair_cols(step, k)
            driven = (inner * step_k).astype(BF)
            st = state[rr, cc]
            zz = z[rr, cc]
            sz = sigmoid(zz)
            act = zz * sz
            gated = st * act
            dns = dmix[rr, mc]
            gk = gain[:, cc]
            mixed_ref[rr, mc] = (gated * scale_s * gk).astype(BF)
            dgated = scale_s * gk * dns - gated * coef
            dgain_ref[:, cc] += jnp.sum(dns * gated * scale_s, axis=0, keepdims=True)
            dz_ref[rr, cc] = (dgated * st * silu_slope(zz, sz)).astype(BF)
            dst = dgated * act
            dr2 = split_pair(dst).astype(BF)
            dmixing = nt(dr2, driven)
            mix = []
            for i, h in enumerate((2 * k, 2 * k + 1)):
                gap = head_col(cum, h) - cum_t[h : h + 1, :]
                decay = jnp.exp(jnp.where(allowed, gap, NEG))
                mix.append((decay * inter).astype(BF))
                dinter = dinter + (dmixing[rows_of(i)] * decay).astype(BF).astype(F32)
            ddriven = tn(jnp.concatenate(mix, axis=0), dr2)
            sk = skip[:, cc]
            dinner = ddriven * step_k + sk * dst
            dskip_ref[:, cc] += jnp.sum(dst * inner, axis=0, keepdims=True)
            dr = dst.astype(BF).astype(F32)
            cross = dr * (st - sk * inner) - driven.astype(F32) * ddriven
            dcum = dcum + nn_exact(cross, heads[cc])
            dstep = dstep + nn_exact(ddriven * inner, heads[cc])
            dcv = dinner * silu_slope(c, sc)
            dv, dk = conv_back(dcv, u[rr, cc], mk[:, cc], pos[rr])
            du_ref[rr, cc] = dv.astype(BF)
            for t in range(KC):
                dmk_ref[t : t + 1, cc] += dk[t]
        dib = dinter.astype(BF)
        blocks[2] = tn(dib, c_out)
        blocks[3] = nn(dib, b_in)
        drate = nn_exact(up, dcum)
        dstep = dstep + drate * rate[...]
        dlog_ref[...] += jnp.sum(drate * step, axis=0, keepdims=True) * rate[...]
        dw = dstep * sigmoid(sin)
        dw_ref[rr] = dw.astype(BF)
        dbias_ref[...] += jnp.sum(dw, axis=0, keepdims=True)
        for i in range(2):
            keep_ref[i, rr] = blocks[r ^ (2 * i)]
            send_ref[i, rr] = blocks[r ^ (2 * i + 1)].astype(BF)


def rss_body(keep, recv, s0_ref, s2_ref):
    for j in range(SLOTS):
        rr, other = rows_of(j), rows_of(j ^ 1)
        s0_ref[rr] = keep[0, rr] + recv[0, other].astype(F32)
        s2_ref[rr] = (keep[1, rr] + recv[1, other].astype(F32)).astype(BF)


def dproj_body(
    scal, s0, recv, raw, pos, cs, sn, kc, dq, dz, du, dw, w,
    dp_ref, send_ref, keep_ref, dkc_ref,
):
    r = scal[0]
    dkc_ref[...] = jnp.zeros_like(dkc_ref)
    for j in range(SLOTS):
        rr = rows_of(j)
        d = s0[rr] + recv[rows_of(j ^ 2)].astype(F32)
        rotated = d * cs[rr] - swap_halves(d) * sn[rr]
        v = raw[rr]
        cv = conv(v, kc[...], pos[rr])
        dcv = d * silu_slope(cv, sigmoid(cv))
        dv, dk = conv_back(dcv, v, kc[...], pos[rr])
        out = jnp.where(r == 0, rotated, jnp.where(r >= 2, dv, d))
        dp_ref[rr, 128:256] = out.astype(BF)
        for t in range(KC):
            dkc_ref[t : t + 1, :] += jnp.where(r >= 2, dk[t], 0.0)
    dp_ref[:, 0:128] = dq[...]
    dp_ref[:, 256:640] = dz[...]
    dp_ref[:, 640:1024] = du[...]
    dp_ref[:, 1024:1030] = dw[:, 0:6]
    for c in range(4):
        cc = slice(c * 256, (c + 1) * 256)
        part = nt(dp_ref[:, 0:1024], w[cc, 0:1024]) + nt(dp_ref[:, 1024:1030], w[cc, 1024:1030])
        for i in range(2):
            keep_ref[i, :, cc] = part[rows_of(2 * i)]
            send_ref[i, :, cc] = part[rows_of(2 * i + 1)].astype(BF)


def dx_body(s0, recv, dm, x, inv, gain, o_ref, gg_ref):
    dn = s0[...] + recv[...].astype(F32)
    xf = x[...].astype(F32)
    i1 = inv[:, 0:1]
    g = gain[...]
    inner = jnp.sum(dn * g * xf, axis=1, keepdims=True)
    o_ref[...] = (dm[...] + i1 * g * dn - xf * (i1 * i1 * i1 * inner / D)).astype(BF)
    gg_ref[...] = jnp.sum(dn * xf * i1, axis=0, keepdims=True)


def kernel(body, outs, args, scal=None, scratch=(), flops=0, mib=40):
    shapes = [jax.ShapeDtypeStruct(s, d) for s, d in outs]
    moved = sum(a.size * a.dtype.itemsize for a in (*args, *shapes))
    vm = pl.BlockSpec(memory_space=pltpu.VMEM)
    specs = [vm] * len(args)
    if scal is not None:
        specs = [pl.BlockSpec(memory_space=pltpu.SMEM), *specs]
        args = (scal, *args)
    return pl.pallas_call(
        body,
        out_shape=shapes,
        in_specs=specs,
        out_specs=[vm] * len(outs),
        scratch_shapes=list(scratch),
        compiler_params=pltpu.CompilerParams(vmem_limit_bytes=mib << 20),
        cost_estimate=pl.CostEstimate(flops=flops, bytes_accessed=moved, transcendentals=0),
    )(*args)


def xor_row(v, k):
    return lax.ppermute(v, "row", [(i, i ^ k) for i in range(SLOTS)])


def gather_row(v):
    a = xor_row(v, 1)
    b = xor_row(v, 2)
    return v, a, b, xor_row(b, 1)


def scatter_row(send, keep):
    recv = xor_row(send, 1)
    width = keep.shape[2]
    s0, s2 = kernel(rsa_body, [((T, width), F32), ((T, width), BF)], (keep, recv), mib=16)
    return s0, xor_row(s2, 2)


def per_device(
    inputs,
    cotangent,
    mixer_in,
    mixer_out,
    expand_weight,
    shrink_weight,
    input_gain,
    middle_gain,
    mixer_kernel,
    shared_kernel,
    decay_log,
    step_bias,
    skip_scale,
    state_gain,
    dealing,
    lengths,
):
    groups = lax.axis_size("dp")
    g = lax.axis_index("dp")
    r = lax.axis_index("row")
    c = lax.axis_index("col")

    def gather_col(v):
        return lax.all_gather(v, "col", axis=0, tiled=True)

    w_in = gather_col(mixer_in)
    w_out = gather_col(mixer_out).reshape(4, 512, 256)
    w_ex = gather_col(expand_weight)
    w_sh = gather_col(shrink_weight).reshape(4, 512, 256)
    gains = lax.all_gather(jnp.stack([input_gain, middle_gain]), "col", axis=1, tiled=True)
    gain1, gain2 = gains[0:1], gains[1:2]

    ids = jnp.arange(groups, dtype=jnp.int32)
    deal_mine = lax.dynamic_index_in_dim(
        lax.dynamic_index_in_dim(dealing, c, 0, False), r, 0, False
    )
    source = jnp.sum(jnp.where(deal_mine == g, ids, 0))
    target = jnp.sum(jnp.where(ids == g, deal_mine, 0))

    def over_dp(v, wanted):
        if groups == 2:
            return v, lax.ppermute(v, "dp", [(0, 1), (1, 0)])
        whole = lax.all_gather(v, "dp", axis=0, tiled=False)
        sel = lax.dynamic_index_in_dim(whole, wanted, 0, False)
        return sel, sel

    scal = jnp.stack(
        [r, (source == g).astype(jnp.int32), (target == g).astype(jnp.int32), c]
    ).astype(jnp.int32)

    def deal_in(v):
        mine = lax.all_to_all(v.reshape(MB, T, 256), "col", split_axis=0, concat_axis=0, tiled=True)
        return over_dp(mine, source)

    def deal_out(v):
        own, peer = over_dp(v, target)
        sel = jnp.where(scal[2] == 1, own, peer) if groups == 2 else own
        parts = jnp.transpose(sel.reshape(T, 4, 256), (1, 0, 2))
        back = lax.all_to_all(parts, "col", split_axis=0, concat_axis=0, tiled=True)
        return back.reshape(MB * T, 256)

    own_x, peer_x = deal_in(inputs)
    x, n1, inv1 = kernel(
        prep_body,
        [((T, D), BF), ((T, D), BF), ((T, 128), F32)],
        (own_x, peer_x, gain1),
        scal,
        mib=16,
    )
    own_y, peer_y = deal_in(cotangent)
    dy = jnp.transpose(jnp.where(scal[1] == 1, own_y, peer_y), (1, 0, 2)).reshape(T, D)

    slot_ids = r ^ jnp.arange(SLOTS, dtype=jnp.int32)
    group_lengths = lax.dynamic_index_in_dim(
        lax.dynamic_index_in_dim(lengths, c, 0, False), g, 0, False
    )
    here = slot_ids[:, None] == jnp.arange(SLOTS, dtype=jnp.int32)[None, :]
    lens = jnp.sum(jnp.where(here[:, :, None], group_lengths[None], 0), axis=1)
    count = lens.shape[1]
    before = jnp.arange(count)[:, None] >= jnp.arange(count)[None, :]
    ends = jnp.sum(jnp.where(before[None], lens[:, None, :], 0), axis=2)
    places = jnp.arange(T, dtype=jnp.int32)
    past = places[None, :, None] >= ends[:, None, :]
    position = places[None, :] - jnp.sum(jnp.where(past, lens[:, None, :], 0), axis=2)
    posf = position.reshape(TT).astype(F32)
    pos = jnp.broadcast_to(posf[:, None], (TT, 128))
    freq = ROPE_BASE ** (-jnp.arange(32, dtype=F32) * 2.0 / HEAD_WIDTH)
    angle = posf[:, None] * freq[None, :]
    cosine, sine = jnp.cos(angle), jnp.sin(angle)
    cs = jnp.concatenate([cosine] * 4, axis=1)
    sn = jnp.concatenate([-sine, sine, -sine, sine], axis=1)
    kernel_start = jnp.clip(r - 2, 0, 1) * 128
    kc = lax.dynamic_slice_in_dim(shared_kernel, kernel_start, 128, 1)

    def pad_lanes(v):
        return jnp.pad(v, (0, 128 - v.shape[0]))[None, :]

    rate = pad_lanes(-jnp.exp(decay_log))
    bias = pad_lanes(step_bias)
    skip = jnp.repeat(skip_scale, MD)[None, :]
    sgain = state_gain[None, :]

    xs = gather_row(n1)
    xcat, q, raw, sh = kernel(
        proj1_body,
        [((TT, D), BF), ((TT, 128), BF), ((TT, 128), F32), ((TT, 128), BF)],
        (*xs, w_in, pos, cs, sn, kc),
        scal,
        flops=2 * TT * D * 256,
    )
    ps = gather_row(sh)
    z, u, wi, cv = kernel(
        proj2_body,
        [((TT, IW), F32), ((TT, IW), F32), ((TT, 128), F32), ((TT, IW), F32)],
        (xcat, w_in, pos, mixer_kernel, bias),
        flops=2 * TT * D * 774,
    )
    ys = gather_row(dy)
    att, prob, state, send, keep = kernel(
        mixf_body,
        [
            ((TT, 128), BF),
            ((2 * TT, 128), F32),
            ((TT, IW), F32),
            ((2, T, 2176), BF),
            ((2, T, 2176), F32),
        ],
        (q, *ps, pos, z, cv, wi, rate, skip, sgain, w_out),
        scal,
        scratch=(pltpu.VMEM((TT, IW), BF), pltpu.VMEM((TT, 128), F32)),
        flops=2 * TT * 512 * D + 10**9,
    )
    s0, got = scatter_row(send, keep)
    mid, n2, zs, inv2 = kernel(
        mid_body,
        [((T, D), F32), ((T, 1152), BF), ((T, D), F32), ((T, 128), F32)],
        (s0, got, x, gain2),
        mib=16,
    )
    ns = gather_row(n2)
    x2, ycat, isb, hidden, dexp, send, keep = kernel(
        ffn_body,
        [
            ((TT, D), BF),
            ((TT, D), BF),
            ((TT, 128), F32),
            ((TT, HW), BF),
            ((TT, 2 * HW), BF),
            ((2, T, D), BF),
            ((2, T, D), F32),
        ],
        (*ns, *ys, w_ex, w_sh),
        flops=5 * TT * D * D,
    )
    s0, got = scatter_row(send, keep)
    dm, db, g_middle = kernel(
        dmid_body,
        [((T, D), F32), ((T, 1152), BF), ((1, D), F32)],
        (s0, got, mid, inv2, dy, gain2, zs),
        mib=16,
    )
    bs = gather_row(db)
    send, keep = kernel(
        outp_body,
        [((2, T, D), BF), ((2, T, D), F32)],
        (hidden, w_sh),
        flops=2 * TT * HW * D,
        mib=16,
    )
    s0, got = scatter_row(send, keep)
    (out,) = kernel(fin_body, [((T, D), BF)], (s0, got, mid), mib=16)
    outputs = deal_out(out)

    def reduce_col(v):
        return lax.psum_scatter(v.astype(BF), "col", scatter_dimension=0, tiled=True)

    g_shrink = reduce_col(tn(ycat, hidden))
    g_expand = reduce_col(tn(x2, dexp))

    (
        dcat, mixed, dq, dz, du, dw, send, keep, g_mk, g_sgain, g_skip, g_log, g_bias,
    ) = kernel(
        mixb_body,
        [
            ((TT, D), BF),
            ((TT, HW), BF),
            ((TT, 128), BF),
            ((TT, IW), BF),
            ((TT, IW), BF),
            ((TT, 128), BF),
            ((2, TT, 128), BF),
            ((2, TT, 128), F32),
            ((KC, IW), F32),
            ((1, IW), F32),
            ((1, IW), F32),
            ((1, 128), F32),
            ((1, 128), F32),
        ],
        (
            *bs, q, *ps, pos, cs, sn, prob, z, u, cv, state, wi, isb,
            att, rate, skip, sgain, mixer_kernel, w_out,
        ),
        scal,
        scratch=(pltpu.VMEM((TT, HW), F32), pltpu.VMEM((4, T, T), F32)),
        flops=2 * TT * 512 * D + 2 * 10**9,
    )
    recv = xor_row(send, 1)
    s0, s2 = kernel(rss_body, [((TT, 128), F32), ((TT, 128), BF)], (keep, recv), mib=16)
    got = xor_row(s2, 2)
    g_out = reduce_col(tn(dcat, mixed))
    dproj, send, keep, g_kc = kernel(
        dproj_body,
        [((TT, 1030), BF), ((2, T, D), BF), ((2, T, D), F32), ((KC, 128), F32)],
        (s0, got, raw, pos, cs, sn, kc, dq, dz, du, dw, w_in),
        scal,
        flops=2 * TT * D * 1030,
    )
    g_in = reduce_col(tn(xcat, dproj))
    s0, got = scatter_row(send, keep)
    dx, g_input = kernel(
        dx_body, [((T, D), BF), ((1, D), F32)], (s0, got, dm, x, inv1, gain1), mib=16
    )
    input_grad = deal_out(dx)

    def sum_dp(v):
        if groups == 2:
            return v.astype(F32) + lax.ppermute(v, "dp", [(0, 1), (1, 0)]).astype(F32)
        return lax.psum(v, "dp").astype(F32)

    grad_in = sum_dp(g_in)
    grad_out = sum_dp(g_out).T
    grad_expand = sum_dp(g_expand)
    grad_shrink = sum_dp(g_shrink).T

    local = jnp.concatenate(
        [g_mk.reshape(-1), g_sgain.reshape(-1), g_skip.reshape(-1), g_log[0], g_bias[0]]
    )
    span = local.shape[0]
    slots = jnp.where(jnp.arange(SLOTS)[:, None] == r, local[None, :], 0.0).reshape(-1)
    kc_cols = jnp.where(jnp.arange(2)[:, None, None] == (r - 2), g_kc[None], 0.0)
    small = jnp.concatenate([slots, g_input[0], g_middle[0], kc_cols.reshape(-1)])
    small = small.reshape(-1, 128)
    if groups == 2:
        small = small + lax.ppermute(small, "dp", [(0, 1), (1, 0)])
        for k in (1, 2):
            small = small + lax.ppermute(small, "col", [(i, i ^ k) for i in range(4)])
        for k in (1, 2):
            small = small + xor_row(small, k)
    else:
        small = lax.psum(small, ("dp", "row", "col"))
    small = small.reshape(-1)
    local = lax.dynamic_slice_in_dim(small, r * span, span, 0)
    rest = small[SLOTS * span :]
    mine = c * 256
    return (
        outputs,
        input_grad,
        grad_in,
        grad_out,
        grad_expand,
        grad_shrink,
        lax.dynamic_slice_in_dim(rest[0:D], mine, 256, 0),
        lax.dynamic_slice_in_dim(rest[D : 2 * D], mine, 256, 0),
        local[0 : KC * IW].reshape(KC, IW),
        jnp.transpose(rest[2 * D :].reshape(2, KC, 128), (1, 0, 2)).reshape(KC, 256),
        local[KC * IW + 2 * IW : KC * IW + 2 * IW + 6],
        local[KC * IW + 2 * IW + 128 : KC * IW + 2 * IW + 134],
        jnp.sum(local[KC * IW + IW : KC * IW + 2 * IW].reshape(6, MD), axis=1),
        local[KC * IW : KC * IW + IW],
    )


def solution(mesh):
    in_specs = (
        P(("dp", "row"), "col"),
        P(("dp", "row"), "col"),
        P("col", "row"),
        P("row", "col"),
        P("col", "row"),
        P("row", "col"),
        P("col"),
        P("col"),
        P(None, "row"),
        P(),
        P("row"),
        P("row"),
        P("row"),
        P("row"),
        P(),
        P(),
    )
    out_specs = (
        P(("dp", "row"), "col"),
        P(("dp", "row"), "col"),
        P("col", "row"),
        P("row", "col"),
        P("col", "row"),
        P("row", "col"),
        P("col"),
        P("col"),
        P(None, "row"),
        P(),
        P("row"),
        P("row"),
        P("row"),
        P("row"),
    )
    return jax.shard_map(
        per_device, mesh=mesh, in_specs=in_specs, out_specs=out_specs, check_vma=False
    )
```
